256 devices in a mesh: tm: 32 (over y, z), space: 8 (over x, core).
Axes of the slice: x: 4, y: 4, z: 8, core: 2. Of those that a mesh axis runs over, the one named last changes fastest.
Arguments:
- inverse_factor: bfloat16 [2, 32, 4096, 4096], P(None, 'tm', 'space'), may hold values from -1.5 to 1.5, as said below
- tile_mask: int32 [32, 32], replicated, may hold values 0 or 1
- carry_rate: float32 [32, 4096, 2], P('tm', 'space'), may hold values from 0 to 1
- right_side: float32 [32, 4096, 2, 128], P('tm', 'space'), may hold values from -1.5 to 1.5
- arrow_rows: bfloat16 [32, 4096, 2, 512], P('tm', 'space'), may hold values from -0.0625 to 0.0625
- fixed_rhs: float32 [2, 512, 128], P(None, ('tm', 'space')), may hold values from -6 to 6
- tip_factor: bfloat16 [2, 512, 512], replicated, may hold values from -1 to 1, as said below
Outputs:
- solution: float32 [32, 4096, 2, 128], P('tm', 'space')
- fixed_solution: float32 [2, 512, 128], P(None, ('tm', 'space'))
The draws below stay inside these ranges and needn't reach their ends.
Inputs may be any that keep to these rules, and one draw needn't show every extreme that they name: `tile_mask`: 1 marks a tile that may be nonzero. `inverse_factor`: only entries on or below the diagonal are read. `tip_factor`: only entries on or below the diagonal are read.
All inputs are finite; a program needn't handle non-finite values.
Results may differ from the reference program's by a relative error of at most 0.022.
Values may be sent and summed in bfloat16 or wider, within the bound.
No kernel may reach another device: no remote copies, remote signals or barrier semaphores. Data moves between devices by JAX's collectives and lax.ppermute only.
A program may use at most 320 MiB of HBM per device.

```python
import math
import jax
import jax.numpy as jnp
from jax import lax

SPATIAL_NODES = 4096
TILE = 128
F = 512
HYPER_SETTINGS = 2
K = 128
TIMES = 32
TILES = 32


def draw_carry_rate(key, part):
    split_keys = jax.random.split(key, 6)
    slow_share = 0.5
    slow_nodes = jax.random.uniform(split_keys[0], (1, SPATIAL_NODES, HYPER_SETTINGS)) < slow_share
    kept_share = jax.random.uniform(split_keys[1], (1, SPATIAL_NODES, HYPER_SETTINGS), minval=0.25, maxval=0.6)
    jitter = jax.random.uniform(split_keys[2], (TIMES, SPATIAL_NODES, HYPER_SETTINGS), minval=0.5, maxval=1.5)
    gradual_rate = jnp.exp(jnp.log(kept_share) * jitter / TIMES)
    place_indices = jax.random.randint(split_keys[3], (2, 1, 1, HYPER_SETTINGS), 1, TIMES)
    temporal_index = jnp.arange(TIMES)[None, :, None, None]
    sudden_rows = jnp.any(place_indices == temporal_index, axis=0)
    sudden_loss = jax.random.uniform(split_keys[4], (1, SPATIAL_NODES, HYPER_SETTINGS), minval=0.65, maxval=0.8)
    fast_rate = jax.random.uniform(split_keys[5], (TIMES, SPATIAL_NODES, HYPER_SETTINGS), minval=0.1, maxval=0.6)
    gradual_portion = gradual_rate * jnp.where(sudden_rows, sudden_loss, 1.0)
    return jnp.where(slow_nodes, gradual_portion, fast_rate).astype(jnp.float32)


def triangular_block(block_key, order, diag_low, diag_high, spread):
    noise_key, diag_key = jax.random.split(block_key)
    noise_vals = jnp.clip(jax.random.normal(noise_key, (order, order)), -5.0, 5.0)
    diagonal = jax.random.uniform(diag_key, (order, 1), minval=diag_low, maxval=diag_high)
    place_indices = jnp.arange(order)
    on_diagonal = place_indices[:, None] == place_indices[None, :]
    return jnp.where(on_diagonal, diagonal, noise_vals * (spread / math.sqrt(order))).astype(jnp.bfloat16)


def draw_inverse_factor(key, part):

    def one_block(block_index):
        return triangular_block(jax.random.fold_in(key, block_index), SPATIAL_NODES, 0.6, 1.4, 1.2)
    blocks = lax.map(one_block, jnp.arange(HYPER_SETTINGS * TIMES))
    return blocks.reshape(HYPER_SETTINGS, TIMES, SPATIAL_NODES, SPATIAL_NODES)


def draw_tip_factor(key, part):

    def one_block(block_index):
        return triangular_block(jax.random.fold_in(key, block_index + 7919), F, 0.35, 0.7, 0.5)
    return lax.map(one_block, jnp.arange(HYPER_SETTINGS))


def with_ends(array, rng, smallest, largest):
    longest = array.shape.index(max(array.shape))
    spots = []
    for shift in (0, 1):
        where = [jax.random.randint(jax.random.fold_in(rng, axis), (), 0, length) for axis, length in enumerate(array.shape)]
        where[longest] = (where[longest] + shift) % array.shape[longest]
        spots.append(tuple(where))
    return array.at[spots[0]].set(smallest).at[spots[1]].set(largest)


def level_of(stream_key, shape, pieces, least, high):
    loudness, own = 1.0, jax.random.fold_in(stream_key, 6)
    for axis_at, parts in pieces:
        draws = jnp.exp(jax.random.uniform(jax.random.fold_in(own, axis_at), (parts,), jnp.float32, least / len(pieces), high / len(pieces)))
        loudness = loudness * jnp.repeat(draws, shape[axis_at] // parts).reshape([-1 if axis == axis_at else 1 for axis in range(len(shape))])
    return loudness


def scatter_about(own_key, dims, deviation, bound, shards=(), kind=jnp.bfloat16):
    result = deviation * jax.random.normal(own_key, dims, jnp.float32)
    if shards:
        result = result * level_of(own_key, dims, shards, -0.22, 0.18)
    return jnp.clip(result, -bound, bound).astype(kind)


def setup_inputs(seed: int = 0) -> dict:
    key_of = jax.random.split(jax.random.key(seed), 8)
    inverse_factor = draw_inverse_factor(jax.random.fold_in(key_of[7], 71), 0)
    tile_mask = with_ends((jax.random.randint(key_of[1], (TILES, TILES), 0, 2) < 1).astype(jnp.int32), jax.random.fold_in(key_of[1], 1), 0, 1)
    carry_rate = draw_carry_rate(jax.random.fold_in(key_of[7], 71), 0)
    right_side = scatter_about(key_of[3], (TIMES, SPATIAL_NODES, HYPER_SETTINGS, K), 0.25, 1.5, ((0, 32), (1, 8)), jnp.float32)
    arrow_rows = scatter_about(key_of[4], (TIMES, SPATIAL_NODES, HYPER_SETTINGS, F), (4.0 * (TIMES * SPATIAL_NODES) ** -0.5), 0.0625, ((0, 32), (1, 8)))
    fixed_rhs = scatter_about(key_of[5], (HYPER_SETTINGS, F, K), 1.0, 6.0, ((1, 256),), jnp.float32)
    tip_factor = draw_tip_factor(jax.random.fold_in(key_of[7], 71), 0)
    return {"inverse_factor": inverse_factor, "tile_mask": tile_mask, "carry_rate": carry_rate, "right_side": right_side, "arrow_rows": arrow_rows, "fixed_rhs": fixed_rhs, "tip_factor": tip_factor}


def kept_cells(tile_mask):
    tile_count = tile_mask.shape[0]
    marked = jnp.maximum(tile_mask, jnp.eye(tile_count, dtype=jnp.int32))
    expanded = jnp.repeat(jnp.repeat(marked, TILE, axis=0), TILE, axis=1)
    place_indices = jnp.arange(SPATIAL_NODES, dtype=jnp.int32)
    return (expanded > 0) & (place_indices[:, None] >= place_indices[None, :])


def reference(inverse_factor, tile_mask, carry_rate, right_side, arrow_rows, fixed_rhs, tip_factor):
    highest = lax.Precision.HIGHEST
    kept = kept_cells(tile_mask)

    def forward_step(carried_value, inputs):
        rate_now, source = inputs
        current = source + rate_now[:, :, None] * carried_value
        return current, current

    _, forward = lax.scan(forward_step, jnp.zeros((SPATIAL_NODES, HYPER_SETTINGS, K), jnp.float32), (carry_rate, right_side))
    forward_b = lax.optimization_barrier(forward.astype(jnp.bfloat16))

    def block_step(block_index):
        factor = lax.dynamic_index_in_dim(inverse_factor, block_index, 1, keepdims=False)
        factor = jnp.where(kept[None], factor, jnp.zeros((), jnp.bfloat16)).astype(jnp.float32)
        vector = lax.dynamic_index_in_dim(forward_b, block_index, 0, keepdims=False).astype(jnp.float32)
        inner_rows = jnp.einsum('hij,jhk->ihk', factor, vector, precision=highest).astype(jnp.bfloat16)
        inner_rows = lax.optimization_barrier(inner_rows).astype(jnp.float32)
        scaled = jnp.einsum('hij,ihk->jhk', factor, inner_rows, precision=highest)
        arrow_part = lax.dynamic_index_in_dim(arrow_rows, block_index, 0, keepdims=False).astype(jnp.float32)
        coupling = jnp.einsum('shf,shk->hfk', arrow_part, vector, precision=highest)
        return scaled, coupling

    scaled, coupling = lax.map(block_step, jnp.arange(TIMES, dtype=jnp.int32))
    fixed_forward = (fixed_rhs - jnp.sum(coupling, axis=0)).astype(jnp.bfloat16)
    fixed_forward = lax.optimization_barrier(fixed_forward).astype(jnp.float32)
    fixed_index = jnp.arange(F, dtype=jnp.int32)
    lower_tri = fixed_index[:, None] >= fixed_index[None, :]
    tip_lower = jnp.where(lower_tri[None], tip_factor, jnp.zeros((), jnp.bfloat16)).astype(jnp.float32)
    tip_inner = jnp.einsum('hij,hjk->hik', tip_lower, fixed_forward, precision=highest).astype(jnp.bfloat16)
    tip_inner = lax.optimization_barrier(tip_inner).astype(jnp.float32)
    fixed_solution = jnp.einsum('hij,hik->hjk', tip_lower, tip_inner, precision=highest)
    fixed_b = lax.optimization_barrier(fixed_solution.astype(jnp.bfloat16)).astype(jnp.float32)

    def carried_step(block_index):
        arrow_part = lax.dynamic_index_in_dim(arrow_rows, block_index, 0, keepdims=False).astype(jnp.float32)
        scaled_now = lax.dynamic_index_in_dim(scaled, block_index, 0, keepdims=False)
        return scaled_now - jnp.einsum('shf,hfk->shk', arrow_part, fixed_b, precision=highest)

    carried = lax.map(carried_step, jnp.arange(TIMES, dtype=jnp.int32))

    def backward_step(passed, inputs):
        rate_now, carried_now = inputs
        current = carried_now + passed
        return rate_now[:, :, None] * current, current

    _, solution = lax.scan(backward_step, jnp.zeros((SPATIAL_NODES, HYPER_SETTINGS, K), jnp.float32), (carry_rate, carried), reverse=True)
    return solution, fixed_solution
```

```python
import functools
import jax
import jax.numpy as jnp
from jax import lax
from jax.experimental import pallas as pl
from jax.experimental.pallas import tpu as pltpu
from jax.sharding import PartitionSpec as P

TILE = 128
BF = jnp.bfloat16
F32 = jnp.float32
MIB = 1 << 20
SHIFTS = (0, 1, 3, 2)


def call(kernel, outs, scratch=(), in_specs=None, vmem=32, flops=1 << 20, moved=1 << 20):
    extra = {} if in_specs is None else {"in_specs": in_specs}
    return pl.pallas_call(
        kernel,
        out_shape=outs,
        scratch_shapes=list(scratch),
        compiler_params=pltpu.CompilerParams(vmem_limit_bytes=vmem * MIB),
        cost_estimate=pl.CostEstimate(flops=flops, bytes_accessed=moved, transcendentals=0),
        **extra,
    )


def shape(dims, kind):
    return jax.ShapeDtypeStruct(dims, kind)


def pack_kernel(side_ref, rate_ref, out_ref):
    blocks, _, lanes = out_ref.shape
    count = side_ref.shape[0] // 2
    per = count // blocks
    for h in range(2):
        rows = side_ref[pl.ds(h, count, stride=2), :]
        out_ref[:, h * per : (h + 1) * per, :] = rows.reshape(blocks, per, lanes).astype(BF)
    rate = rate_ref[...]
    high = rate.astype(BF).astype(F32)
    middle = (rate - high).astype(BF).astype(F32)
    low = rate - high - middle
    terms = jnp.concatenate([high, middle, low, jnp.zeros_like(low)], axis=0)
    shared = lanes // per
    for group in range(count // lanes):
        part = terms[:, group * lanes : (group + 1) * lanes].astype(BF)
        out_ref[group * shared : (group + 1) * shared, 2 * per :, :] = jnp.broadcast_to(
            part[None], (shared,) + part.shape
        )


def forward_kernel(got_ref, out_ref, rate_ref, rows_ref, turn_ref):
    times, height, lanes = got_ref.shape
    per = (height - 8) // 2
    rows_ref[...] = got_ref[:, 2 * per :, :].astype(F32).reshape(times * 8, lanes)
    parts = []
    for h in range(2):
        terms = [rows_ref[pl.ds(2 * k + h, times, stride=8), :] for k in range(3)]
        parts.append(terms[0] + terms[1] + terms[2])
    filler = jnp.zeros((lanes - 2 * times, lanes), F32)
    turn_ref[...] = jnp.transpose(jnp.concatenate(parts + [filler], axis=0))
    place = lax.axis_index("tm")
    start = pl.multiple_of(lax.rem(place, lanes // per) * per, per)
    rate = turn_ref[pl.ds(start, per), :]
    rate_ref[...] = rate
    current = got_ref[0, : 2 * per, :].astype(F32)
    out_ref[0] = current.astype(BF)
    for t in range(1, times):
        now = jnp.concatenate(
            [
                jnp.broadcast_to(rate[:, h * times + t : h * times + t + 1], (per, lanes))
                for h in range(2)
            ],
            axis=0,
        )
        current = got_ref[t, : 2 * per, :].astype(F32) + now * current
        out_ref[t] = current.astype(BF)


def backward_kernel(got_ref, rate_ref, out_ref):
    times, height, lanes = got_ref.shape
    per = height // 2
    rate = rate_ref[...]
    following = jnp.zeros((height, lanes), F32)
    out_ref[times - 1] = following.astype(BF)
    for t in range(times - 2, -1, -1):
        now = jnp.concatenate(
            [
                jnp.broadcast_to(rate[:, h * times + t + 1 : h * times + t + 2], (per, lanes))
                for h in range(2)
            ],
            axis=0,
        )
        following = now * (got_ref[t + 1].astype(F32) + following)
        out_ref[t] = following.astype(BF)


def setting_rows(ref, h):
    blocks, height, lanes = ref.shape
    per = height // 2
    return ref[:, h * per : (h + 1) * per, :].reshape(blocks * per, lanes)


def coupling_kernel(arrow_ref, forward_ref, out_ref):
    blocks, height, lanes = out_ref.shape
    per = height // 2
    for h in range(2):
        total = lax.dot_general(
            arrow_ref[h],
            setting_rows(forward_ref, h),
            (((0,), (0,)), ((), ())),
            preferred_element_type=F32,
        )
        out_ref[:, h * per : (h + 1) * per, :] = (-total).astype(BF).reshape(blocks, per, lanes)


def sum_kernel(got_ref, rhs_ref, out_ref):
    times, height, lanes = got_ref.shape
    total = got_ref[0].astype(F32)
    for t in range(1, times):
        total = total + got_ref[t].astype(F32)
    out_ref[...] = total
    own = rhs_ref.shape[1]
    place = lax.axis_index("space") * own
    for h in range(2):
        rows = pl.ds(h * (height // 2) + place, own)
        out_ref[rows, :] = out_ref[rows, :] + rhs_ref[h]


def tip_kernel(fixed_ref, tip_ref, full_ref, own_ref, solved_ref):
    order = tip_ref.shape[1]
    row = lax.broadcasted_iota(jnp.int32, (order, order), 0)
    col = lax.broadcasted_iota(jnp.int32, (order, order), 1)
    own = own_ref.shape[1]
    place = (lax.axis_index("tm") * lax.axis_size("space") + lax.axis_index("space")) * own
    for h in range(2):
        lower = jnp.where(row >= col, tip_ref[h].astype(F32), 0.0).astype(BF)
        inner = jnp.dot(lower, setting_rows(fixed_ref, h), preferred_element_type=F32).astype(BF)
        solved = lax.dot_general(
            lower, inner, (((0,), (0,)), ((), ())), preferred_element_type=F32
        )
        solved_ref[...] = solved
        full_ref[h] = solved.astype(BF)
        own_ref[h] = solved_ref[pl.ds(place, own), :]


def factor_kernel(mask_ref, *refs):
    pieces = refs[:8]
    factor_ref, keep_ref, send_ref, held, total, sems = refs[8:]
    rows = total.shape[1]
    per = pieces[0].shape[1] // 2
    blocks = pieces[0].shape[0]
    tiles = rows // TILE
    place = lax.axis_index("space")
    chip, core = place // 2, lax.rem(place, 2)

    def index_of(e, shift):
        return 2 * lax.rem(chip + shift, 4) + (1 - core if e else core)

    sources = [index_of(e, 4 - shift) for e in range(2) for shift in SHIFTS]

    def copy(j):
        start = pl.multiple_of(sources[j] * rows, rows)
        return pltpu.make_async_copy(
            factor_ref.at[:, :, pl.ds(start, rows)], held.at[j], sems.at[j]
        )

    for j in range(8):

        @pl.when(sources[j] <= place)
        def _(j=j):
            copy(j).start()

    total[...] = jnp.zeros_like(total)
    for j in range(8):

        @pl.when(sources[j] <= place)
        def _(j=j):
            copy(j).wait()

            @pl.loop(0, tiles * tiles)
            def _(at):
                r, c = at // tiles, lax.rem(at, tiles)
                marked = mask_ref[place * tiles + r, sources[j] * tiles + c] > 0
                dead = jnp.logical_not(marked)
                if j == 0:
                    dead = jnp.logical_or(jnp.logical_and(dead, r != c), r < c)

                @pl.when(dead)
                def _():
                    rs = pl.ds(pl.multiple_of(r * TILE, TILE), TILE)
                    cs = pl.ds(pl.multiple_of(c * TILE, TILE), TILE)
                    held[j, :, rs, cs] = jnp.zeros((2, TILE, TILE), BF)

            if j == 0:
                row = lax.broadcasted_iota(jnp.int32, (TILE, TILE), 0)
                col = lax.broadcasted_iota(jnp.int32, (TILE, TILE), 1)
                for h in range(2):
                    for r in range(tiles):
                        sl = slice(r * TILE, (r + 1) * TILE)
                        block = held[0, h, sl, sl].astype(F32)
                        held[0, h, sl, sl] = jnp.where(row >= col, block, 0.0).astype(BF)
            for h in range(2):
                total[h] += jnp.dot(
                    held[j, h], setting_rows(pieces[j], h), preferred_element_type=F32
                )

    for e, out_ref in ((1, send_ref), (0, keep_ref)):
        for d, shift in enumerate(SHIFTS):
            target = index_of(e, shift)
            at = 4 * e + SHIFTS.index((4 - shift) % 4)

            @pl.when(target <= place)
            def _(at=at, d=d, out_ref=out_ref):
                for h in range(2):
                    got = lax.dot_general(
                        held[at, h],
                        total[h].astype(BF),
                        (((0,), (0,)), ((), ())),
                        preferred_element_type=F32,
                    )
                    out_ref[d, :, h * per : (h + 1) * per, :] = got.astype(BF).reshape(
                        blocks, per, TILE
                    )

            @pl.when(target > place)
            def _(d=d, out_ref=out_ref):
                out_ref[d] = jnp.zeros(out_ref.shape[1:], BF)


def add_kernel(keep_ref, got_ref, *outs):
    for d, out_ref in enumerate(outs):
        out_ref[...] = (keep_ref[d].astype(F32) + got_ref[d].astype(F32)).astype(BF)


def carried_kernel(a_ref, b_ref, c_ref, d_ref, arrow_ref, fixed_ref, carried_ref, out_ref):
    blocks, height, lanes = a_ref.shape
    per = height // 2
    for h in range(2):
        total = setting_rows(a_ref, h).astype(F32)
        for ref in (b_ref, c_ref, d_ref):
            total = total + setting_rows(ref, h).astype(F32)
        total = total - jnp.dot(arrow_ref[h], fixed_ref[h], preferred_element_type=F32)
        carried_ref[h] = total
        out_ref[:, h * per : (h + 1) * per, :] = total.astype(BF).reshape(blocks, per, lanes)


def final_kernel(carried_ref, following_ref, out_ref):
    count = carried_ref.shape[1]
    for h in range(2):
        out_ref[pl.ds(h, count, stride=2), :] = carried_ref[h] + setting_rows(
            following_ref, h
        ).astype(F32)


def on_device(inverse_factor, tile_mask, carry_rate, right_side, arrow_rows, fixed_rhs, tip_factor):
    times = lax.axis_size("tm")
    devices = lax.axis_size("space")
    _, count, _, lanes = right_side.shape
    per = count // times
    block = (times, 2 * per, lanes)
    fixed_total = tip_factor.shape[1]
    near = [(i, i + 1 - 2 * (i % 2)) for i in range(devices)]

    def along(shift):
        chips = devices // 2
        return [(i, 2 * ((i // 2 + shift) % chips) + i % 2) for i in range(devices)]

    def turned(array):
        return lax.all_to_all(array, "tm", 0, 0, tiled=True)

    arrow = jnp.transpose(arrow_rows[0], (1, 0, 2))
    packed = call(pack_kernel, shape((times, 2 * per + 8, lanes), BF))(
        right_side.reshape(2 * count, lanes), jnp.transpose(carry_rate[0])
    )
    forward, rate = call(
        forward_kernel,
        (shape(block, BF), shape((per, lanes), F32)),
        [pltpu.VMEM((8 * times, lanes), F32), pltpu.VMEM((lanes, lanes), F32)],
    )(turned(packed))
    forward_b = turned(forward)

    pieces = [forward_b] + [lax.ppermute(forward_b, "space", along(s)) for s in SHIFTS[1:]]
    coupling = call(coupling_kernel, shape((times, 2 * fixed_total // times, lanes), BF))(
        arrow, forward_b
    )
    sums = call(sum_kernel, shape((2 * fixed_total // times, lanes), F32))(
        turned(coupling), fixed_rhs
    )
    pieces = pieces + [lax.ppermute(p, "space", near) for p in pieces]
    keep, send = call(
        factor_kernel,
        (shape((4,) + block, BF), shape((4,) + block, BF)),
        [
            pltpu.VMEM((8, 2, count, count), BF),
            pltpu.VMEM((2, count, lanes), F32),
            pltpu.SemaphoreType.DMA((8,)),
        ],
        in_specs=[pl.BlockSpec(memory_space=pltpu.SMEM)]
        + [pl.BlockSpec(memory_space=pltpu.VMEM)] * 8
        + [pl.BlockSpec(memory_space=pl.ANY)],
        vmem=40,
        flops=1 << 31,
        moved=12 * MIB,
    )(tile_mask, *pieces, inverse_factor[:, 0])
    parts = call(add_kernel, (shape(block, BF),) * 4)(keep, lax.ppermute(send, "space", near))
    scaled = [parts[0]] + [lax.ppermute(p, "space", along(s)) for p, s in zip(parts[1:], SHIFTS[1:])]

    sums = sums + lax.ppermute(sums, "space", near)
    fixed = sums
    for s in SHIFTS[1:]:
        fixed = fixed + lax.ppermute(sums, "space", along(s))
    fixed_forward = turned(
        jnp.broadcast_to(fixed.astype(BF)[None], (times,) + fixed.shape)
    )
    fixed_b, fixed_own = call(
        tip_kernel,
        (shape((2, fixed_total, lanes), BF), shape(fixed_rhs.shape, F32)),
        [pltpu.VMEM((fixed_total, lanes), F32)],
    )(fixed_forward, tip_factor)

    carried, ready = call(carried_kernel, (shape((2, count, lanes), F32), shape(block, BF)))(
        *scaled, arrow, fixed_b
    )
    following = turned(call(backward_kernel, shape(block, BF))(turned(ready), rate))
    solution = call(final_kernel, shape((2 * count, lanes), F32))(carried, following)
    return (solution.reshape(right_side.shape), fixed_own)


def solution(mesh):
    placed = (
        P(None, "tm", "space", None),
        P(),
        P("tm", "space", None),
        P("tm", "space", None, None),
        P("tm", "space", None, None),
        P(None, ("tm", "space"), None),
        P(),
    )
    return jax.shard_map(
        on_device,
        mesh=mesh,
        in_specs=placed,
        out_specs=(P("tm", "space", None, None), P(None, ("tm", "space"), None)),
        check_vma=False,
    )
```

```python
import functools
import jax
import jax.numpy as jnp
from jax import lax
from jax.experimental import pallas as pl
from jax.experimental.pallas import tpu as pltpu
from jax.sharding import PartitionSpec as P

TILE = 128
BF = jnp.bfloat16
F32 = jnp.float32
MIB = 1 << 20
SHIFTS = (0, 1, 3, 2)


def call(kernel, outs, scratch=(), in_specs=None, out_specs=None, vmem=6, flops=1 << 20, moved=1 << 20):
    extra = {} if in_specs is None else {"in_specs": in_specs}
    if out_specs is not None:
        extra["out_specs"] = out_specs
    return pl.pallas_call(
        kernel,
        out_shape=outs,
        scratch_shapes=list(scratch),
        compiler_params=pltpu.CompilerParams(vmem_limit_bytes=vmem * MIB),
        cost_estimate=pl.CostEstimate(flops=flops, bytes_accessed=moved, transcendentals=0),
        **extra,
    )


def shape(dims, kind):
    return jax.ShapeDtypeStruct(dims, kind)


def pack_kernel(side_ref, rate_ref, out_ref):
    blocks, _, lanes = out_ref.shape
    count = side_ref.shape[0] // 2
    per = count // blocks
    for h in range(2):
        rows = side_ref[pl.ds(h, count, stride=2), :]
        out_ref[:, h * per : (h + 1) * per, :] = rows.reshape(blocks, per, lanes).astype(BF)
    rate = rate_ref[...]
    high = rate.astype(BF).astype(F32)
    middle = (rate - high).astype(BF).astype(F32)
    low = rate - high - middle
    terms = jnp.concatenate([high, middle, low, jnp.zeros_like(low)], axis=0)
    shared = lanes // per
    for group in range(count // lanes):
        part = terms[:, group * lanes : (group + 1) * lanes].astype(BF)
        out_ref[group * shared : (group + 1) * shared, 2 * per :, :] = jnp.broadcast_to(
            part[None], (shared,) + part.shape
        )


def forward_kernel(got_ref, out_ref, rate_ref, rows_ref, turn_ref):
    times, height, lanes = got_ref.shape
    per = (height - 8) // 2
    rows_ref[...] = got_ref[:, 2 * per :, :].astype(F32).reshape(times * 8, lanes)
    parts = []
    for h in range(2):
        terms = [rows_ref[pl.ds(2 * k + h, times, stride=8), :] for k in range(3)]
        parts.append(terms[0] + terms[1] + terms[2])
    filler = jnp.zeros((lanes - 2 * times, lanes), F32)
    turn_ref[...] = jnp.transpose(jnp.concatenate(parts + [filler], axis=0))
    place = lax.axis_index("tm")
    start = pl.multiple_of(lax.rem(place, lanes // per) * per, per)
    rate = turn_ref[pl.ds(start, per), :]
    rate_ref[...] = rate
    current = got_ref[0, : 2 * per, :].astype(F32)
    out_ref[0] = current.astype(BF)
    for t in range(1, times):
        now = jnp.concatenate(
            [
                jnp.broadcast_to(rate[:, h * times + t : h * times + t + 1], (per, lanes))
                for h in range(2)
            ],
            axis=0,
        )
        current = got_ref[t, : 2 * per, :].astype(F32) + now * current
        out_ref[t] = current.astype(BF)


def backward_kernel(got_ref, rate_ref, out_ref):
    times, height, lanes = got_ref.shape
    per = height // 2
    rate = rate_ref[...]
    following = jnp.zeros((height, lanes), F32)
    out_ref[times - 1] = following.astype(BF)
    for t in range(times - 2, -1, -1):
        now = jnp.concatenate(
            [
                jnp.broadcast_to(rate[:, h * times + t + 1 : h * times + t + 2], (per, lanes))
                for h in range(2)
            ],
            axis=0,
        )
        following = now * (got_ref[t + 1].astype(F32) + following)
        out_ref[t] = following.astype(BF)


def setting_rows(ref, h):
    blocks, height, lanes = ref.shape
    per = height // 2
    return ref[:, h * per : (h + 1) * per, :].reshape(blocks * per, lanes)


def coupling_kernel(arrow_ref, forward_ref, out_ref):
    blocks, height, lanes = out_ref.shape
    per = height // 2
    for h in range(2):
        total = lax.dot_general(
            arrow_ref[h],
            setting_rows(forward_ref, h),
            (((0,), (0,)), ((), ())),
            preferred_element_type=F32,
        )
        out_ref[:, h * per : (h + 1) * per, :] = (-total).astype(BF).reshape(blocks, per, lanes)


def sum_kernel(got_ref, rhs_ref, out_ref):
    times, height, lanes = got_ref.shape
    total = got_ref[0].astype(F32)
    for t in range(1, times):
        total = total + got_ref[t].astype(F32)
    out_ref[...] = total
    own = rhs_ref.shape[1]
    place = lax.axis_index("space") * own
    for h in range(2):
        rows = pl.ds(h * (height // 2) + place, own)
        out_ref[rows, :] = out_ref[rows, :] + rhs_ref[h]


def tip_kernel(fixed_ref, tip_ref, full_ref, own_ref, solved_ref):
    order = tip_ref.shape[1]
    row = lax.broadcasted_iota(jnp.int32, (order, order), 0)
    col = lax.broadcasted_iota(jnp.int32, (order, order), 1)
    own = own_ref.shape[1]
    place = (lax.axis_index("tm") * lax.axis_size("space") + lax.axis_index("space")) * own
    for h in range(2):
        lower = jnp.where(row >= col, tip_ref[h].astype(F32), 0.0).astype(BF)
        inner = jnp.dot(lower, setting_rows(fixed_ref, h), preferred_element_type=F32).astype(BF)
        solved = lax.dot_general(
            lower, inner, (((0,), (0,)), ((), ())), preferred_element_type=F32
        )
        solved_ref[...] = solved
        full_ref[h] = solved.astype(BF)
        own_ref[h] = solved_ref[pl.ds(place, own), :]


def index_of(e, shift):
    place = lax.axis_index("space")
    chip, core = place // 2, lax.rem(place, 2)
    return 2 * lax.rem(chip + shift, 4) + (1 - core if e else core)


def factor_kernel(mask_ref, *refs):
    pieces = refs[:8]
    factor_ref, keep_ref, send_ref, held, values, total, parts, sems = refs[8:]
    rows = held.shape[2]
    tiles = rows // TILE
    place = lax.axis_index("space")
    sources = [index_of(e, 4 - shift) for e in range(2) for shift in SHIFTS]

    def copies(j):
        start = pl.multiple_of(sources[j] * rows, rows)
        return (
            pltpu.make_async_copy(pieces[j], values.at[j], sems.at[0, j]),
            pltpu.make_async_copy(
                factor_ref.at[:, :, pl.ds(start, rows)], held.at[j], sems.at[1, j]
            ),
        )

    def copy_out(e, d):
        out_ref = send_ref if e else keep_ref
        return pltpu.make_async_copy(parts.at[4 * e + d], out_ref.at[d], sems.at[2, 4 * e + d])

    for j in range(8):

        @pl.when(sources[j] <= place)
        def _(j=j):
            for copy in copies(j):
                copy.start()

    total[...] = jnp.zeros_like(total)
    for j in range(8):

        @pl.when(sources[j] <= place)
        def _(j=j):
            for copy in copies(j):
                copy.wait()

            @pl.loop(0, tiles * tiles)
            def _(at):
                r, c = at // tiles, lax.rem(at, tiles)
                marked = mask_ref[place * tiles + r, sources[j] * tiles + c] > 0
                dead = jnp.logical_not(marked)
                if j == 0:
                    dead = jnp.logical_or(jnp.logical_and(dead, r != c), r < c)

                @pl.when(dead)
                def _():
                    rs = pl.ds(pl.multiple_of(r * TILE, TILE), TILE)
                    cs = pl.ds(pl.multiple_of(c * TILE, TILE), TILE)
                    held[j, :, rs, cs] = jnp.zeros((2, TILE, TILE), BF)

            if j == 0:
                row = lax.broadcasted_iota(jnp.int32, (TILE, TILE), 0)
                col = lax.broadcasted_iota(jnp.int32, (TILE, TILE), 1)
                for h in range(2):
                    for r in range(tiles):
                        sl = slice(r * TILE, (r + 1) * TILE)
                        block = held[0, h, sl, sl].astype(F32)
                        held[0, h, sl, sl] = jnp.where(row >= col, block, 0.0).astype(BF)
            for h in range(2):
                total[h] += jnp.dot(
                    held[j, h], setting_rows(values.at[j], h), preferred_element_type=F32
                )

    inner = [jnp.transpose(total[h]).astype(BF) for h in range(2)]
    for e in (1, 0):
        for d, shift in enumerate(SHIFTS):
            target = index_of(e, shift)
            at = 4 * e + SHIFTS.index((4 - shift) % 4)

            @pl.when(target <= place)
            def _(at=at, to=4 * e + d):
                for h in range(2):
                    parts[to, h] = jnp.dot(
                        inner[h], held[at, h], preferred_element_type=F32
                    ).astype(BF)

            @pl.when(target > place)
            def _(to=4 * e + d):
                parts[to] = jnp.zeros(parts.shape[1:], BF)

            copy_out(e, d).start()
    for e in (1, 0):
        for d in range(4):
            copy_out(e, d).wait()


def add_kernel(keep_ref, got_ref, *refs):
    outs = refs[:4]
    kept, other, sems = refs[4:]
    ins = [
        (
            pltpu.make_async_copy(keep_ref.at[d], kept.at[d], sems.at[0, d]),
            pltpu.make_async_copy(got_ref.at[d], other.at[d], sems.at[1, d]),
        )
        for d in range(4)
    ]
    back = [pltpu.make_async_copy(kept.at[d], outs[d], sems.at[2, d]) for d in range(4)]
    order = (3, 1, 2, 0)
    for d in order:
        for copy in ins[d]:
            copy.start()
    for d in order:
        for copy in ins[d]:
            copy.wait()
        kept[d] = (kept[d].astype(F32) + other[d].astype(F32)).astype(BF)
        back[d].start()
    for d in order:
        back[d].wait()


def carried_kernel(a_ref, b_ref, c_ref, d_ref, arrow_ref, fixed_ref, carried_ref, out_ref):
    blocks, height, lanes = out_ref.shape
    per = height // 2
    for h in range(2):
        total = a_ref[h].astype(F32)
        for ref in (b_ref, c_ref, d_ref):
            total = total + ref[h].astype(F32)
        total = jnp.transpose(total)
        total = total - jnp.dot(arrow_ref[h], fixed_ref[h], preferred_element_type=F32)
        carried_ref[h] = total
        out_ref[:, h * per : (h + 1) * per, :] = total.astype(BF).reshape(blocks, per, lanes)


def final_kernel(carried_ref, following_ref, out_ref):
    count = carried_ref.shape[1]
    for h in range(2):
        out_ref[pl.ds(h, count, stride=2), :] = carried_ref[h] + setting_rows(
            following_ref, h
        ).astype(F32)


def on_device(inverse_factor, tile_mask, carry_rate, right_side, arrow_rows, fixed_rhs, tip_factor):
    times = lax.axis_size("tm")
    devices = lax.axis_size("space")
    _, count, _, lanes = right_side.shape
    per = count // times
    block = (times, 2 * per, lanes)
    fixed_total = tip_factor.shape[1]
    near = [(i, i + 1 - 2 * (i % 2)) for i in range(devices)]

    def along(shift):
        chips = devices // 2
        return [(i, 2 * ((i // 2 + shift) % chips) + i % 2) for i in range(devices)]

    def turned(array):
        return lax.all_to_all(array, "tm", 0, 0, tiled=True)

    def distant(array):
        return pltpu.with_memory_space_constraint(array, pltpu.HBM)

    arrow = jnp.transpose(arrow_rows[0], (1, 0, 2))
    packed = call(pack_kernel, shape((times, 2 * per + 8, lanes), BF))(
        right_side.reshape(2 * count, lanes), jnp.transpose(carry_rate[0])
    )
    forward, rate = call(
        forward_kernel,
        (shape(block, BF), shape((per, lanes), F32)),
        [pltpu.VMEM((8 * times, lanes), F32), pltpu.VMEM((lanes, lanes), F32)],
    )(turned(packed))
    forward_b = turned(forward)

    far = pl.BlockSpec(memory_space=pltpu.HBM)
    pieces = [forward_b] + [lax.ppermute(forward_b, "space", along(s)) for s in SHIFTS[1:]]
    coupling = call(coupling_kernel, shape((times, 2 * fixed_total // times, lanes), BF))(
        arrow, forward_b
    )
    sums = call(sum_kernel, shape((2 * fixed_total // times, lanes), F32))(
        turned(coupling), fixed_rhs
    )
    pieces = pieces + [lax.ppermute(p, "space", near) for p in pieces]
    pieces, sums = lax.optimization_barrier((pieces, sums))
    part = (2, lanes, count)
    keep, send = call(
        factor_kernel,
        (shape((4,) + part, BF), shape((4,) + part, BF)),
        [
            pltpu.VMEM((8, 2, count, count), BF),
            pltpu.VMEM((8,) + block, BF),
            pltpu.VMEM((2, count, lanes), F32),
            pltpu.VMEM((8,) + part, BF),
            pltpu.SemaphoreType.DMA((3, 8)),
        ],
        in_specs=[pl.BlockSpec(memory_space=pltpu.SMEM)] + [far] * 9,
        out_specs=(far, far),
        vmem=24,
        flops=1 << 31,
        moved=12 * MIB,
    )(tile_mask, *[distant(p) for p in pieces], distant(inverse_factor[:, 0]))
    parts = call(
        add_kernel,
        (shape(part, BF),) * 4,
        [
            pltpu.VMEM((4,) + part, BF),
            pltpu.VMEM((4,) + part, BF),
            pltpu.SemaphoreType.DMA((3, 4)),
        ],
        in_specs=[far, far],
        out_specs=(far,) * 4,
    )(distant(keep), distant(lax.ppermute(send, "space", near)))
    scaled = [parts[0]] + [lax.ppermute(p, "space", along(s)) for p, s in zip(parts[1:], SHIFTS[1:])]

    sums = sums + lax.ppermute(sums, "space", near)
    fixed = sums
    for s in SHIFTS[1:]:
        fixed = fixed + lax.ppermute(sums, "space", along(s))
    fixed_forward = turned(jnp.broadcast_to(fixed.astype(BF)[None], (times,) + fixed.shape))
    fixed_b, fixed_own = call(
        tip_kernel,
        (shape((2, fixed_total, lanes), BF), shape(fixed_rhs.shape, F32)),
        [pltpu.VMEM((fixed_total, lanes), F32)],
    )(fixed_forward, tip_factor)

    carried, ready = call(carried_kernel, (shape((2, count, lanes), F32), shape(block, BF)))(
        *scaled, arrow, fixed_b
    )
    following = turned(call(backward_kernel, shape(block, BF))(turned(ready), rate))
    solution = call(final_kernel, shape((2 * count, lanes), F32))(carried, following)
    return (solution.reshape(right_side.shape), fixed_own)


def solution(mesh):
    placed = (
        P(None, "tm", "space", None),
        P(),
        P("tm", "space", None),
        P("tm", "space", None, None),
        P("tm", "space", None, None),
        P(None, ("tm", "space"), None),
        P(),
    )
    return jax.shard_map(
        on_device,
        mesh=mesh,
        in_specs=placed,
        out_specs=(P("tm", "space", None, None), P(None, ("tm", "space"), None)),
        check_vma=False,
    )
```

```python
import functools
import jax
import jax.numpy as jnp
from jax import lax
from jax.experimental import pallas as pl
from jax.experimental.pallas import tpu as pltpu
from jax.sharding import PartitionSpec as P

TILE = 128
BF = jnp.bfloat16
F32 = jnp.float32
MIB = 1 << 20
SHIFTS = (0, 1, 3, 2)


def call(kernel, outs, scratch=(), in_specs=None, out_specs=None, vmem=6, flops=1 << 20, moved=1 << 20):
    extra = {} if in_specs is None else {"in_specs": in_specs}
    if out_specs is not None:
        extra["out_specs"] = out_specs
    return pl.pallas_call(
        kernel,
        out_shape=outs,
        scratch_shapes=list(scratch),
        compiler_params=pltpu.CompilerParams(vmem_limit_bytes=vmem * MIB),
        cost_estimate=pl.CostEstimate(flops=flops, bytes_accessed=moved, transcendentals=0),
        **extra,
    )


def shape(dims, kind):
    return jax.ShapeDtypeStruct(dims, kind)


def pack_kernel(side_hbm, rate_hbm, out_ref, side_ref, rate_ref, sems):
    blocks, _, lanes = out_ref.shape
    count = side_ref.shape[0] // 2
    per = count // blocks
    groups = 4
    copies = [pltpu.make_async_copy(rate_hbm, rate_ref, sems.at[groups])]
    for g in range(groups):
        rows = pl.ds(g * (2 * count // groups), 2 * count // groups)
        copies.append(pltpu.make_async_copy(side_hbm.at[rows], side_ref.at[rows], sems.at[g]))
    for copy in copies:
        copy.start()
    copies[0].wait()
    for g in range(groups):
        copies[1 + g].wait()
        first, some = g * (blocks // groups), blocks // groups
        for h in range(2):
            rows = side_ref[pl.ds(2 * first * per + h, some * per, stride=2), :]
            out_ref[first : first + some, h * per : (h + 1) * per, :] = rows.reshape(
                some, per, lanes
            ).astype(BF)
    rate = rate_ref[...]
    high = rate.astype(BF).astype(F32)
    middle = (rate - high).astype(BF).astype(F32)
    low = rate - high - middle
    terms = jnp.concatenate([high, middle, low, jnp.zeros_like(low)], axis=0)
    shared = lanes // per
    for group in range(count // lanes):
        part = terms[:, group * lanes : (group + 1) * lanes].astype(BF)
        out_ref[group * shared : (group + 1) * shared, 2 * per :, :] = jnp.broadcast_to(
            part[None], (shared,) + part.shape
        )


def forward_kernel(got_ref, out_ref, rate_ref, rows_ref, turn_ref):
    times, height, lanes = got_ref.shape
    per = (height - 8) // 2
    rows_ref[...] = got_ref[:, 2 * per :, :].astype(F32).reshape(times * 8, lanes)
    parts = []
    for h in range(2):
        terms = [rows_ref[pl.ds(2 * k + h, times, stride=8), :] for k in range(3)]
        parts.append(terms[0] + terms[1] + terms[2])
    filler = jnp.zeros((lanes - 2 * times, lanes), F32)
    turn_ref[...] = jnp.transpose(jnp.concatenate(parts + [filler], axis=0))
    place = lax.axis_index("tm")
    start = pl.multiple_of(lax.rem(place, lanes // per) * per, per)
    rate = turn_ref[pl.ds(start, per), :]
    rate_ref[...] = rate
    current = got_ref[0, : 2 * per, :].astype(F32)
    out_ref[0] = current.astype(BF)
    for t in range(1, times):
        now = jnp.concatenate(
            [
                jnp.broadcast_to(rate[:, h * times + t : h * times + t + 1], (per, lanes))
                for h in range(2)
            ],
            axis=0,
        )
        current = got_ref[t, : 2 * per, :].astype(F32) + now * current
        out_ref[t] = current.astype(BF)


def backward_kernel(got_ref, rate_ref, out_ref):
    times, height, lanes = got_ref.shape
    per = height // 2
    rate = rate_ref[...]
    following = jnp.zeros((height, lanes), F32)
    out_ref[times - 1] = following.astype(BF)
    for t in range(times - 2, -1, -1):
        now = jnp.concatenate(
            [
                jnp.broadcast_to(rate[:, h * times + t + 1 : h * times + t + 2], (per, lanes))
                for h in range(2)
            ],
            axis=0,
        )
        following = now * (got_ref[t + 1].astype(F32) + following)
        out_ref[t] = following.astype(BF)


def setting_rows(ref, h):
    blocks, height, lanes = ref.shape
    per = height // 2
    return ref[:, h * per : (h + 1) * per, :].reshape(blocks * per, lanes)


def coupling_kernel(arrow_ref, forward_ref, out_ref):
    blocks, height, lanes = out_ref.shape
    per = height // 2
    for h in range(2):
        total = lax.dot_general(
            arrow_ref[h],
            setting_rows(forward_ref, h),
            (((0,), (0,)), ((), ())),
            preferred_element_type=F32,
        )
        out_ref[:, h * per : (h + 1) * per, :] = (-total).astype(BF).reshape(blocks, per, lanes)


def sum_kernel(got_ref, rhs_ref, out_ref):
    times, height, lanes = got_ref.shape
    total = got_ref[0].astype(F32)
    for t in range(1, times):
        total = total + got_ref[t].astype(F32)
    out_ref[...] = total
    own = rhs_ref.shape[1]
    place = lax.axis_index("space") * own
    for h in range(2):
        rows = pl.ds(h * (height // 2) + place, own)
        out_ref[rows, :] = out_ref[rows, :] + rhs_ref[h]


def spread_kernel(a_ref, b_ref, c_ref, d_ref, out_ref):
    total = (a_ref[...] + b_ref[...]) + (c_ref[...] + d_ref[...])
    out_ref[...] = jnp.broadcast_to(total.astype(BF)[None], out_ref.shape)


def tip_kernel(fixed_ref, tip_ref, full_ref, own_ref, solved_ref):
    order = tip_ref.shape[1]
    row = lax.broadcasted_iota(jnp.int32, (order, order), 0)
    col = lax.broadcasted_iota(jnp.int32, (order, order), 1)
    own = own_ref.shape[1]
    place = (lax.axis_index("tm") * lax.axis_size("space") + lax.axis_index("space")) * own
    for h in range(2):
        lower = jnp.where(row >= col, tip_ref[h].astype(F32), 0.0).astype(BF)
        inner = jnp.dot(lower, setting_rows(fixed_ref, h), preferred_element_type=F32).astype(BF)
        solved = lax.dot_general(
            lower, inner, (((0,), (0,)), ((), ())), preferred_element_type=F32
        )
        solved_ref[...] = solved
        full_ref[h] = solved.astype(BF)
        own_ref[h] = solved_ref[pl.ds(place, own), :]


def index_of(e, shift):
    place = lax.axis_index("space")
    chip, core = place // 2, lax.rem(place, 2)
    return 2 * lax.rem(chip + shift, 4) + (1 - core if e else core)


def keep_kernel(mask_ref, factor_ref, out_ref, held, sems):
    rows = held.shape[2]
    tiles = rows // TILE
    place = lax.axis_index("space")
    sources = [index_of(e, 4 - shift) for e in range(2) for shift in SHIFTS]

    def copy_in(j):
        start = pl.multiple_of(sources[j] * rows, rows)
        return pltpu.make_async_copy(
            factor_ref.at[:, :, pl.ds(start, rows)], held.at[j], sems.at[0, j]
        )

    def copy_out(j):
        return pltpu.make_async_copy(held.at[j], out_ref.at[j], sems.at[1, j])

    for j in range(8):

        @pl.when(sources[j] <= place)
        def _(j=j):
            copy_in(j).start()

    for j in range(8):

        @pl.when(sources[j] <= place)
        def _(j=j):
            copy_in(j).wait()

            @pl.loop(0, tiles * tiles)
            def _(at):
                r, c = at // tiles, lax.rem(at, tiles)
                marked = mask_ref[place * tiles + r, sources[j] * tiles + c] > 0
                dead = jnp.logical_not(marked)
                if j == 0:
                    dead = jnp.logical_or(jnp.logical_and(dead, r != c), r < c)

                @pl.when(dead)
                def _():
                    rs = pl.ds(pl.multiple_of(r * TILE, TILE), TILE)
                    cs = pl.ds(pl.multiple_of(c * TILE, TILE), TILE)
                    held[j, :, rs, cs] = jnp.zeros((2, TILE, TILE), BF)

            if j == 0:
                row = lax.broadcasted_iota(jnp.int32, (TILE, TILE), 0)
                col = lax.broadcasted_iota(jnp.int32, (TILE, TILE), 1)
                for h in range(2):
                    for r in range(tiles):
                        sl = slice(r * TILE, (r + 1) * TILE)
                        block = held[0, h, sl, sl].astype(F32)
                        held[0, h, sl, sl] = jnp.where(row >= col, block, 0.0).astype(BF)
            copy_out(j).start()

    for j in range(8):

        @pl.when(sources[j] <= place)
        def _(j=j):
            copy_out(j).wait()


def factor_kernel(*refs):
    pieces = refs[:8]
    factor_ref, keep_ref, send_ref, held, values, total, parts, sems = refs[8:]
    place = lax.axis_index("space")
    sources = [index_of(e, 4 - shift) for e in range(2) for shift in SHIFTS]

    def copies(j):
        return (
            pltpu.make_async_copy(pieces[j], values.at[j], sems.at[0, j]),
            pltpu.make_async_copy(factor_ref.at[j], held.at[j], sems.at[1, j]),
        )

    def copy_out(e, d):
        out_ref = send_ref if e else keep_ref
        return pltpu.make_async_copy(parts.at[4 * e + d], out_ref.at[d], sems.at[2, 4 * e + d])

    for j in range(8):

        @pl.when(sources[j] <= place)
        def _(j=j):
            for copy in copies(j):
                copy.start()

    for j in range(8):

        @pl.when(sources[j] <= place)
        def _(j=j):
            for copy in copies(j):
                copy.wait()
            for h in range(2):
                got = jnp.dot(
                    held[j, h], setting_rows(values.at[j], h), preferred_element_type=F32
                )
                total[h] = total[h] + got if j else got

    inner = [jnp.transpose(total[h]).astype(BF) for h in range(2)]
    for e in (1, 0):
        for d, shift in enumerate(SHIFTS):
            target = index_of(e, shift)
            at = 4 * e + SHIFTS.index((4 - shift) % 4)

            @pl.when(target <= place)
            def _(at=at, to=4 * e + d):
                for h in range(2):
                    parts[to, h] = jnp.dot(
                        inner[h], held[at, h], preferred_element_type=F32
                    ).astype(BF)

            @pl.when(target > place)
            def _(to=4 * e + d):
                parts[to] = jnp.zeros(parts.shape[1:], BF)

            copy_out(e, d).start()
    for e in (1, 0):
        for d in range(4):
            copy_out(e, d).wait()


def add_kernel(keep_ref, got_ref, *refs):
    outs = refs[:4]
    kept, other, sems = refs[4:]
    ins = [
        (
            pltpu.make_async_copy(keep_ref.at[d], kept.at[d], sems.at[0, d]),
            pltpu.make_async_copy(got_ref.at[d], other.at[d], sems.at[1, d]),
        )
        for d in range(4)
    ]
    back = [pltpu.make_async_copy(kept.at[d], outs[d], sems.at[2, d]) for d in range(4)]
    order = (3, 1, 2, 0)
    for d in order:
        for copy in ins[d]:
            copy.start()
    for d in order:
        for copy in ins[d]:
            copy.wait()
        kept[d] = kept[d] + other[d]
        back[d].start()
    for d in order:
        back[d].wait()


def carried_kernel(
    a_hbm, b_ref, c_ref, d_ref, arrow_ref, fixed_ref, carried_ref, out_ref, a_ref, sem
):
    blocks, height, lanes = out_ref.shape
    per = height // 2
    copy = pltpu.make_async_copy(a_hbm, a_ref, sem)
    copy.start()
    for h in range(2):
        total = b_ref[h].astype(F32) + c_ref[h].astype(F32) + d_ref[h].astype(F32)
        if h == 0:
            copy.wait()
        total = jnp.transpose(total + a_ref[h].astype(F32))
        total = total - jnp.dot(arrow_ref[h], fixed_ref[h], preferred_element_type=F32)
        carried_ref[h] = total
        out_ref[:, h * per : (h + 1) * per, :] = total.astype(BF).reshape(blocks, per, lanes)


def final_kernel(carried_ref, following_ref, out_ref):
    count = carried_ref.shape[1]
    for h in range(2):
        out_ref[pl.ds(h, count, stride=2), :] = carried_ref[h] + setting_rows(
            following_ref, h
        ).astype(F32)


def on_device(inverse_factor, tile_mask, carry_rate, right_side, arrow_rows, fixed_rhs, tip_factor):
    times = lax.axis_size("tm")
    devices = lax.axis_size("space")
    _, count, _, lanes = right_side.shape
    per = count // times
    block = (times, 2 * per, lanes)
    fixed_total = tip_factor.shape[1]
    near = [(i, i + 1 - 2 * (i % 2)) for i in range(devices)]

    def along(shift):
        chips = devices // 2
        return [(i, 2 * ((i // 2 + shift) % chips) + i % 2) for i in range(devices)]

    def turned(array):
        return lax.all_to_all(array, "tm", 0, 0, tiled=True)

    def distant(array):
        return pltpu.with_memory_space_constraint(array, pltpu.HBM)

    far = pl.BlockSpec(memory_space=pltpu.HBM)
    packed = call(
        pack_kernel,
        shape((times, 2 * per + 8, lanes), BF),
        [
            pltpu.VMEM((2 * count, lanes), F32),
            pltpu.VMEM((2, count), F32),
            pltpu.SemaphoreType.DMA((5,)),
        ],
        in_specs=[far, far],
    )(distant(right_side.reshape(2 * count, lanes)), distant(jnp.transpose(carry_rate[0])))
    packed, tile_mask = lax.optimization_barrier((packed, tile_mask))
    held = call(
        keep_kernel,
        pltpu.HBM((8, 2, count, count), BF),
        [pltpu.VMEM((8, 2, count, count), BF), pltpu.SemaphoreType.DMA((2, 8))],
        in_specs=[pl.BlockSpec(memory_space=pltpu.SMEM), far],
        out_specs=far,
        vmem=12,
        moved=16 * MIB,
    )(tile_mask, distant(inverse_factor[:, 0]))
    packed, held = lax.optimization_barrier((turned(packed), held))
    forward, rate = call(
        forward_kernel,
        (shape(block, BF), shape((per, lanes), F32)),
        [pltpu.VMEM((8 * times, lanes), F32), pltpu.VMEM((lanes, lanes), F32)],
    )(packed)
    forward_b = turned(forward)

    pieces = [forward_b] + [lax.ppermute(forward_b, "space", along(s)) for s in SHIFTS[1:]]
    arrow_rows, forward_b = lax.optimization_barrier((arrow_rows, forward_b))
    arrow = jnp.transpose(arrow_rows[0], (1, 0, 2))
    coupling = call(
        coupling_kernel,
        shape((times, 2 * fixed_total // times, lanes), BF),
        flops=1 << 32,
        moved=8 * MIB,
    )(arrow, forward_b)
    sums = call(sum_kernel, shape((2 * fixed_total // times, lanes), F32))(
        turned(coupling), fixed_rhs
    )
    pieces = pieces + [lax.ppermute(p, "space", near) for p in pieces]
    sums = sums + lax.ppermute(sums, "space", near)
    pieces, sums = lax.optimization_barrier((pieces, sums))
    fixed = [sums] + [lax.ppermute(sums, "space", along(s)) for s in SHIFTS[1:]]
    part = (2, lanes, count)
    keep, send = call(
        factor_kernel,
        (pltpu.HBM((4,) + part, BF), pltpu.HBM((4,) + part, BF)),
        [
            pltpu.VMEM((8, 2, count, count), BF),
            pltpu.VMEM((8,) + block, BF),
            pltpu.VMEM((2, count, lanes), F32),
            pltpu.VMEM((8,) + part, BF),
            pltpu.SemaphoreType.DMA((3, 8)),
        ],
        in_specs=[far] * 9,
        out_specs=(far, far),
        vmem=24,
        flops=1 << 31,
        moved=12 * MIB,
    )(*[distant(p) for p in pieces], distant(held))
    spread = call(spread_kernel, shape((times,) + sums.shape, BF))(*fixed)
    send, spread = lax.optimization_barrier((send, spread))
    parts = call(
        add_kernel,
        (pltpu.HBM(part, BF),) * 4,
        [
            pltpu.VMEM((4,) + part, BF),
            pltpu.VMEM((4,) + part, BF),
            pltpu.SemaphoreType.DMA((3, 4)),
        ],
        in_specs=[far, far],
        out_specs=(far,) * 4,
    )(distant(keep), distant(lax.ppermute(send, "space", near)))
    scaled = [parts[0]] + [lax.ppermute(p, "space", along(s)) for p, s in zip(parts[1:], SHIFTS[1:])]

    fixed_b, fixed_own = call(
        tip_kernel,
        (shape((2, fixed_total, lanes), BF), shape(fixed_rhs.shape, F32)),
        [pltpu.VMEM((fixed_total, lanes), F32)],
    )(turned(spread), tip_factor)

    carried, ready = call(
        carried_kernel,
        (shape((2, count, lanes), F32), shape(block, BF)),
        [pltpu.VMEM(part, BF), pltpu.SemaphoreType.DMA],
        in_specs=[far] + [pl.BlockSpec(memory_space=pltpu.VMEM)] * 5,
    )(distant(scaled[0]), *scaled[1:], arrow, fixed_b)
    following = turned(call(backward_kernel, shape(block, BF))(turned(ready), rate))
    solution = call(final_kernel, shape((2 * count, lanes), F32))(carried, following)
    return (solution.reshape(right_side.shape), fixed_own)


def solution(mesh):
    placed = (
        P(None, "tm", "space", None),
        P(),
        P("tm", "space", None),
        P("tm", "space", None, None),
        P("tm", "space", None, None),
        P(None, ("tm", "space"), None),
        P(),
    )
    return jax.shard_map(
        on_device,
        mesh=mesh,
        in_specs=placed,
        out_specs=(P("tm", "space", None, None), P(None, ("tm", "space"), None)),
        check_vma=False,
    )
```

```python
import functools
import jax
import jax.numpy as jnp
from jax import lax
from jax.experimental import pallas as pl
from jax.experimental.pallas import tpu as pltpu
from jax.sharding import PartitionSpec as P

TILE = 128
BF = jnp.bfloat16
F32 = jnp.float32
MIB = 1 << 20
SHIFTS = (0, 1, 3, 2)


def call(kernel, outs, scratch=(), in_specs=None, out_specs=None, vmem=6, flops=1 << 20, moved=1 << 20):
    extra = {} if in_specs is None else {"in_specs": in_specs}
    if out_specs is not None:
        extra["out_specs"] = out_specs
    return pl.pallas_call(
        kernel,
        out_shape=outs,
        scratch_shapes=list(scratch),
        compiler_params=pltpu.CompilerParams(vmem_limit_bytes=vmem * MIB),
        cost_estimate=pl.CostEstimate(flops=flops, bytes_accessed=moved, transcendentals=0),
        **extra,
    )


def shape(dims, kind):
    return jax.ShapeDtypeStruct(dims, kind)


def pack_kernel(side_hbm, rate_hbm, out_ref, side_ref, rate_ref, sems):
    blocks, _, lanes = out_ref.shape
    count = side_ref.shape[0] // 2
    per = count // blocks
    groups = 4
    copies = [pltpu.make_async_copy(rate_hbm, rate_ref, sems.at[groups])]
    for g in range(groups):
        rows = pl.ds(g * (2 * count // groups), 2 * count // groups)
        copies.append(pltpu.make_async_copy(side_hbm.at[rows], side_ref.at[rows], sems.at[g]))
    for copy in copies:
        copy.start()
    copies[0].wait()
    for g in range(groups):
        copies[1 + g].wait()
        first, some = g * (blocks // groups), blocks // groups
        for h in range(2):
            rows = side_ref[pl.ds(2 * first * per + h, some * per, stride=2), :]
            out_ref[first : first + some, h * per : (h + 1) * per, :] = rows.reshape(
                some, per, lanes
            ).astype(BF)
    rate = rate_ref[...]
    high = rate.astype(BF).astype(F32)
    middle = (rate - high).astype(BF).astype(F32)
    low = rate - high - middle
    terms = jnp.concatenate([high, middle, low, jnp.zeros_like(low)], axis=0)
    shared = lanes // per
    for group in range(count // lanes):
        part = terms[:, group * lanes : (group + 1) * lanes].astype(BF)
        out_ref[group * shared : (group + 1) * shared, 2 * per :, :] = jnp.broadcast_to(
            part[None], (shared,) + part.shape
        )


def forward_kernel(got_ref, out_ref, rate_ref, rows_ref, turn_ref):
    times, height, lanes = got_ref.shape
    per = (height - 8) // 2
    rows_ref[...] = got_ref[:, 2 * per :, :].astype(F32).reshape(times * 8, lanes)
    parts = []
    for h in range(2):
        terms = [rows_ref[pl.ds(2 * k + h, times, stride=8), :] for k in range(3)]
        parts.append(terms[0] + terms[1] + terms[2])
    filler = jnp.zeros((lanes - 2 * times, lanes), F32)
    turn_ref[...] = jnp.transpose(jnp.concatenate(parts + [filler], axis=0))
    place = lax.axis_index("tm")
    start = pl.multiple_of(lax.rem(place, lanes // per) * per, per)
    rate = turn_ref[pl.ds(start, per), :]
    rate_ref[...] = rate
    current = got_ref[0, : 2 * per, :].astype(F32)
    out_ref[0] = current.astype(BF)
    for t in range(1, times):
        now = jnp.concatenate(
            [
                jnp.broadcast_to(rate[:, h * times + t : h * times + t + 1], (per, lanes))
                for h in range(2)
            ],
            axis=0,
        )
        current = got_ref[t, : 2 * per, :].astype(F32) + now * current
        out_ref[t] = current.astype(BF)


def backward_kernel(got_ref, rate_ref, out_ref):
    times, height, lanes = got_ref.shape
    per = height // 2
    rate = rate_ref[...]
    following = jnp.zeros((height, lanes), F32)
    out_ref[times - 1] = following.astype(BF)
    for t in range(times - 2, -1, -1):
        now = jnp.concatenate(
            [
                jnp.broadcast_to(rate[:, h * times + t + 1 : h * times + t + 2], (per, lanes))
                for h in range(2)
            ],
            axis=0,
        )
        following = now * (got_ref[t + 1].astype(F32) + following)
        out_ref[t] = following.astype(BF)


def setting_rows(ref, h):
    blocks, height, lanes = ref.shape
    per = height // 2
    return ref[:, h * per : (h + 1) * per, :].reshape(blocks * per, lanes)


def coupling_kernel(arrow_ref, forward_ref, out_ref):
    blocks, height, lanes = out_ref.shape
    per = height // 2
    for h in range(2):
        total = lax.dot_general(
            arrow_ref[h],
            setting_rows(forward_ref, h),
            (((0,), (0,)), ((), ())),
            preferred_element_type=F32,
        )
        out_ref[:, h * per : (h + 1) * per, :] = (-total).astype(BF).reshape(blocks, per, lanes)


def sum_kernel(got_ref, rhs_ref, out_ref):
    times, height, lanes = got_ref.shape
    total = got_ref[0].astype(F32)
    for t in range(1, times):
        total = total + got_ref[t].astype(F32)
    out_ref[...] = total
    own = rhs_ref.shape[1]
    place = lax.axis_index("space") * own
    for h in range(2):
        rows = pl.ds(h * (height // 2) + place, own)
        out_ref[rows, :] = out_ref[rows, :] + rhs_ref[h]


def settle_kernel(a_ref, b_ref, c_ref, d_ref, out_ref):
    rows = out_ref.shape[0]
    total = (a_ref[...] + b_ref[...]) + (c_ref[...] + d_ref[...])
    first = lax.rem(lax.axis_index("space"), 2) == 0
    out_ref[...] = jnp.where(first, total[:rows], total[rows:]).astype(BF)


def spread_kernel(*refs):
    out_ref = refs[-1]
    line = jnp.concatenate([ref[...] for ref in refs[:-1]], axis=0)
    out_ref[...] = jnp.broadcast_to(line[None], out_ref.shape)


def tip_kernel(got_ref, tip_ref, mine_ref, own_ref, other_ref, solved_ref, fixed_ref):
    order = tip_ref.shape[1]
    line, high, lanes = got_ref.shape
    rows = order // (line * (lax.axis_size("tm") // line))
    lines = high // rows
    outer = lax.axis_index("tm") // line
    for d in range(lines):
        start = lax.rem(outer + lines - d, lines) * line
        fixed_ref[pl.ds(start, line)] = got_ref[:, d * rows : (d + 1) * rows, :]
    core = lax.rem(lax.axis_index("space"), 2)
    row = lax.broadcasted_iota(jnp.int32, (order, order), 0)
    col = lax.broadcasted_iota(jnp.int32, (order, order), 1)
    lower = jnp.where(row >= col, tip_ref[core].astype(F32), 0.0).astype(BF)
    fixed = fixed_ref[...].reshape(order, lanes)
    inner = jnp.dot(lower, fixed, preferred_element_type=F32).astype(BF)
    solved = lax.dot_general(lower, inner, (((0,), (0,)), ((), ())), preferred_element_type=F32)
    solved_ref[...] = solved
    mine_ref[...] = solved.astype(BF)
    own = own_ref.shape[0]
    place = lax.axis_index("tm") * lax.axis_size("space") + lax.axis_index("space")
    own_ref[...] = solved_ref[pl.ds(place * own, own), :]
    other_ref[...] = solved_ref[pl.ds((place + 1 - 2 * core) * own, own), :]


def index_of(e, shift):
    place = lax.axis_index("space")
    chip, core = place // 2, lax.rem(place, 2)
    return 2 * lax.rem(chip + shift, 4) + (1 - core if e else core)


def keep_kernel(mask_ref, factor_ref, out_ref, held, sems):
    rows = held.shape[2]
    tiles = rows // TILE
    place = lax.axis_index("space")
    sources = [index_of(e, 4 - shift) for e in range(2) for shift in SHIFTS]

    def copy_in(j):
        start = pl.multiple_of(sources[j] * rows, rows)
        return pltpu.make_async_copy(
            factor_ref.at[:, :, pl.ds(start, rows)], held.at[j], sems.at[0, j]
        )

    def copy_out(j):
        return pltpu.make_async_copy(held.at[j], out_ref.at[j], sems.at[1, j])

    for j in range(8):

        @pl.when(sources[j] <= place)
        def _(j=j):
            copy_in(j).start()

    for j in range(8):

        @pl.when(sources[j] <= place)
        def _(j=j):
            copy_in(j).wait()

            @pl.loop(0, tiles * tiles)
            def _(at):
                r, c = at // tiles, lax.rem(at, tiles)
                marked = mask_ref[place * tiles + r, sources[j] * tiles + c] > 0
                dead = jnp.logical_not(marked)
                if j == 0:
                    dead = jnp.logical_or(jnp.logical_and(dead, r != c), r < c)

                @pl.when(dead)
                def _():
                    rs = pl.ds(pl.multiple_of(r * TILE, TILE), TILE)
                    cs = pl.ds(pl.multiple_of(c * TILE, TILE), TILE)
                    held[j, :, rs, cs] = jnp.zeros((2, TILE, TILE), BF)

            if j == 0:
                row = lax.broadcasted_iota(jnp.int32, (TILE, TILE), 0)
                col = lax.broadcasted_iota(jnp.int32, (TILE, TILE), 1)
                for h in range(2):
                    for r in range(tiles):
                        sl = slice(r * TILE, (r + 1) * TILE)
                        block = held[0, h, sl, sl].astype(F32)
                        held[0, h, sl, sl] = jnp.where(row >= col, block, 0.0).astype(BF)
            copy_out(j).start()

    for j in range(8):

        @pl.when(sources[j] <= place)
        def _(j=j):
            copy_out(j).wait()


def factor_kernel(*refs):
    pieces = refs[:8]
    factor_ref, keep_ref, send_ref, held, values, total, parts, sems = refs[8:]
    place = lax.axis_index("space")
    sources = [index_of(e, 4 - shift) for e in range(2) for shift in SHIFTS]

    def copies(j):
        return (
            pltpu.make_async_copy(pieces[j], values.at[j], sems.at[0, j]),
            pltpu.make_async_copy(factor_ref.at[j], held.at[j], sems.at[1, j]),
        )

    def copy_out(e, d):
        out_ref = send_ref if e else keep_ref
        return pltpu.make_async_copy(parts.at[4 * e + d], out_ref.at[d], sems.at[2, 4 * e + d])

    for j in range(8):

        @pl.when(sources[j] <= place)
        def _(j=j):
            for copy in copies(j):
                copy.start()

    for j in range(8):

        @pl.when(sources[j] <= place)
        def _(j=j):
            for copy in copies(j):
                copy.wait()
            for h in range(2):
                got = jnp.dot(
                    held[j, h], setting_rows(values.at[j], h), preferred_element_type=F32
                )
                total[h] = total[h] + got if j else got

    inner = [jnp.transpose(total[h]).astype(BF) for h in range(2)]
    for e in (1, 0):
        for d, shift in enumerate(SHIFTS):
            target = index_of(e, shift)
            at = 4 * e + SHIFTS.index((4 - shift) % 4)

            @pl.when(target <= place)
            def _(at=at, to=4 * e + d):
                for h in range(2):
                    parts[to, h] = jnp.dot(
                        inner[h], held[at, h], preferred_element_type=F32
                    ).astype(BF)

            @pl.when(target > place)
            def _(to=4 * e + d):
                parts[to] = jnp.zeros(parts.shape[1:], BF)

            copy_out(e, d).start()
    for e in (1, 0):
        for d in range(4):
            copy_out(e, d).wait()


def add_kernel(keep_ref, got_ref, *outs):
    for d, out_ref in enumerate(outs):
        out_ref[...] = keep_ref[d] + got_ref[d]


def carried_kernel(
    a_ref, b_ref, c_ref, d_ref, arrow_ref, mine_ref, other_ref, own_ref, got_ref,
    carried_ref, out_ref, both_ref, fixed_ref
):
    blocks, height, lanes = out_ref.shape
    per = height // 2
    core = lax.rem(lax.axis_index("space"), 2)
    fixed_ref[pl.ds(core, 1)] = mine_ref[...][None]
    fixed_ref[pl.ds(1 - core, 1)] = other_ref[...][None]
    both_ref[pl.ds(core, 1)] = own_ref[...][None]
    both_ref[pl.ds(1 - core, 1)] = got_ref[...][None]
    for h in range(2):
        total = (a_ref[h].astype(F32) + b_ref[h].astype(F32)) + (
            c_ref[h].astype(F32) + d_ref[h].astype(F32)
        )
        total = jnp.transpose(total)
        total = total - jnp.dot(arrow_ref[h], fixed_ref[h], preferred_element_type=F32)
        carried_ref[h] = total
        out_ref[:, h * per : (h + 1) * per, :] = total.astype(BF).reshape(blocks, per, lanes)


def final_kernel(carried_ref, following_ref, out_ref):
    count = carried_ref.shape[1]
    for h in range(2):
        out_ref[pl.ds(h, count, stride=2), :] = carried_ref[h] + setting_rows(
            following_ref, h
        ).astype(F32)


def on_device(inverse_factor, tile_mask, carry_rate, right_side, arrow_rows, fixed_rhs, tip_factor):
    times = lax.axis_size("tm")
    devices = lax.axis_size("space")
    _, count, _, lanes = right_side.shape
    per = count // times
    block = (times, 2 * per, lanes)
    fixed_total = tip_factor.shape[1]
    near = [(i, i + 1 - 2 * (i % 2)) for i in range(devices)]

    def along(shift):
        chips = devices // 2
        return [(i, 2 * ((i // 2 + shift) % chips) + i % 2) for i in range(devices)]

    def turned(array):
        return lax.all_to_all(array, "tm", 0, 0, tiled=True)

    def distant(array):
        return pltpu.with_memory_space_constraint(array, pltpu.HBM)

    far = pl.BlockSpec(memory_space=pltpu.HBM)
    packed = call(
        pack_kernel,
        shape((times, 2 * per + 8, lanes), BF),
        [
            pltpu.VMEM((2 * count, lanes), F32),
            pltpu.VMEM((2, count), F32),
            pltpu.SemaphoreType.DMA((5,)),
        ],
        in_specs=[far, far],
    )(distant(right_side.reshape(2 * count, lanes)), distant(jnp.transpose(carry_rate[0])))
    packed, tile_mask = lax.optimization_barrier((packed, tile_mask))
    held = call(
        keep_kernel,
        pltpu.HBM((8, 2, count, count), BF),
        [pltpu.VMEM((8, 2, count, count), BF), pltpu.SemaphoreType.DMA((2, 8))],
        in_specs=[pl.BlockSpec(memory_space=pltpu.SMEM), far],
        out_specs=far,
        vmem=12,
        moved=16 * MIB,
    )(tile_mask, distant(inverse_factor[:, 0]))
    packed, held = lax.optimization_barrier((turned(packed), held))
    forward, rate = call(
        forward_kernel,
        (shape(block, BF), shape((per, lanes), F32)),
        [pltpu.VMEM((8 * times, lanes), F32), pltpu.VMEM((lanes, lanes), F32)],
    )(packed)
    forward_b = turned(forward)

    pieces = [forward_b] + [lax.ppermute(forward_b, "space", along(s)) for s in SHIFTS[1:]]
    arrow_rows, forward_b = lax.optimization_barrier((arrow_rows, forward_b))
    arrow = jnp.transpose(arrow_rows[0], (1, 0, 2))
    coupling = call(
        coupling_kernel,
        shape((times, 2 * fixed_total // times, lanes), BF),
        flops=1 << 32,
        moved=8 * MIB,
    )(arrow, forward_b)
    sums = call(sum_kernel, shape((2 * fixed_total // times, lanes), F32))(
        turned(coupling), fixed_rhs
    )
    pieces = pieces + [lax.ppermute(p, "space", near) for p in pieces]
    sums = sums + lax.ppermute(sums, "space", near)
    pieces, sums = lax.optimization_barrier((pieces, sums))
    fixed = [sums] + [lax.ppermute(sums, "space", along(s)) for s in SHIFTS[1:]]
    part = (2, lanes, count)
    keep, send = call(
        factor_kernel,
        (shape((4,) + part, BF), shape((4,) + part, BF)),
        [
            pltpu.VMEM((8, 2, count, count), BF),
            pltpu.VMEM((8,) + block, BF),
            pltpu.VMEM((2, count, lanes), F32),
            pltpu.VMEM((8,) + part, BF),
            pltpu.SemaphoreType.DMA((3, 8)),
        ],
        in_specs=[far] * 9,
        out_specs=(far, far),
        vmem=24,
        flops=1 << 31,
        moved=12 * MIB,
    )(*[distant(p) for p in pieces], distant(held))
    chunk = (sums.shape[0] // 2, lanes)
    settled = call(settle_kernel, shape(chunk, BF))(*fixed)
    send, settled = lax.optimization_barrier((send, settled))
    parts = call(add_kernel, (shape(part, BF),) * 4, vmem=8)(keep, lax.ppermute(send, "space", near))

    line = 8
    lines = times // line
    inner = [[y * line + z for z in range(line)] for y in range(lines)]
    chunks = [settled]
    for d in range(1, lines):
        pairs = [(i, (i + d * line) % times) for i in range(times)]
        chunks.append(lax.ppermute(settled, "tm", pairs))
    chunks, parts = lax.optimization_barrier((chunks, parts))
    scaled = [parts[0]] + [lax.ppermute(p, "space", along(s)) for p, s in zip(parts[1:], SHIFTS[1:])]
    spread = call(spread_kernel, shape((line, lines * chunk[0], lanes), BF))(*chunks)
    got = lax.all_to_all(spread, "tm", 0, 0, axis_index_groups=inner, tiled=True)
    own = (fixed_rhs.shape[1], lanes)
    mine, own_rows, other_rows = call(
        tip_kernel,
        (shape((fixed_total, lanes), BF), shape(own, F32), shape(own, F32)),
        [pltpu.VMEM((fixed_total, lanes), F32), pltpu.VMEM((times,) + chunk, BF)],
    )(got, tip_factor)
    carried, ready, fixed_own = call(
        carried_kernel,
        (shape((2, count, lanes), F32), shape(block, BF), shape(fixed_rhs.shape, F32)),
        [pltpu.VMEM((2, fixed_total, lanes), BF)],
    )(
        *scaled,
        arrow,
        mine,
        lax.ppermute(mine, "space", near),
        own_rows,
        lax.ppermute(other_rows, "space", near),
    )
    following = turned(call(backward_kernel, shape(block, BF))(turned(ready), rate))
    solution = call(final_kernel, shape((2 * count, lanes), F32))(carried, following)
    return (solution.reshape(right_side.shape), fixed_own)


def solution(mesh):
    placed = (
        P(None, "tm", "space", None),
        P(),
        P("tm", "space", None),
        P("tm", "space", None, None),
        P("tm", "space", None, None),
        P(None, ("tm", "space"), None),
        P(),
    )
    return jax.shard_map(
        on_device,
        mesh=mesh,
        in_specs=placed,
        out_specs=(P("tm", "space", None, None), P(None, ("tm", "space"), None)),
        check_vma=False,
    )
```

```python
import functools
import jax
import jax.numpy as jnp
from jax import lax
from jax.experimental import pallas as pl
from jax.experimental.pallas import tpu as pltpu
from jax.sharding import PartitionSpec as P

TILE = 128
BF = jnp.bfloat16
F32 = jnp.float32
MIB = 1 << 20
SHIFTS = (0, 1, 3, 2)


def call(kernel, outs, scratch=(), in_specs=None, out_specs=None, vmem=6, flops=1 << 20, moved=1 << 20):
    extra = {} if in_specs is None else {"in_specs": in_specs}
    if out_specs is not None:
        extra["out_specs"] = out_specs
    return pl.pallas_call(
        kernel,
        out_shape=outs,
        scratch_shapes=list(scratch),
        compiler_params=pltpu.CompilerParams(vmem_limit_bytes=vmem * MIB),
        cost_estimate=pl.CostEstimate(flops=flops, bytes_accessed=moved, transcendentals=0),
        **extra,
    )


def shape(dims, kind):
    return jax.ShapeDtypeStruct(dims, kind)


def pack_kernel(side_hbm, rate_hbm, out_hbm, side_ref, rate_ref, out_ref, sems):
    blocks, _, lanes = out_ref.shape
    count = side_ref.shape[0] // 2
    per = count // blocks
    groups, some = count // lanes, lanes // per
    copies = [pltpu.make_async_copy(rate_hbm, rate_ref, sems.at[2 * groups])]
    for g in range(groups):
        rows = pl.ds(g * 2 * lanes, 2 * lanes)
        copies.append(pltpu.make_async_copy(side_hbm.at[rows], side_ref.at[rows], sems.at[g]))
    for copy in copies:
        copy.start()
    copies[0].wait()
    rate = rate_ref[...]
    high = rate.astype(BF).astype(F32)
    middle = (rate - high).astype(BF).astype(F32)
    low = rate - high - middle
    terms = jnp.concatenate([high, middle, low, jnp.zeros_like(low)], axis=0)
    back = []
    for g in range(groups):
        copies[1 + g].wait()
        here = slice(g * some, (g + 1) * some)
        for h in range(2):
            rows = side_ref[pl.ds(2 * g * lanes + h, lanes, stride=2), :]
            out_ref[here, h * per : (h + 1) * per, :] = rows.reshape(some, per, lanes).astype(BF)
        part = terms[:, g * lanes : (g + 1) * lanes].astype(BF)
        out_ref[here, 2 * per :, :] = jnp.broadcast_to(part[None], (some,) + part.shape)
        span = pl.ds(g * some, some)
        back.append(
            pltpu.make_async_copy(out_ref.at[span], out_hbm.at[span], sems.at[groups + g])
        )
        back[g].start()
    for copy in back:
        copy.wait()


def forward_kernel(got_ref, out_ref, rate_ref, rows_ref, turn_ref):
    times, height, lanes = got_ref.shape
    per = (height - 8) // 2
    rows_ref[...] = got_ref[:, 2 * per :, :].astype(F32).reshape(times * 8, lanes)
    parts = []
    for h in range(2):
        terms = [rows_ref[pl.ds(2 * k + h, times, stride=8), :] for k in range(3)]
        parts.append(terms[0] + terms[1] + terms[2])
    filler = jnp.zeros((lanes - 2 * times, lanes), F32)
    turn_ref[...] = jnp.transpose(jnp.concatenate(parts + [filler], axis=0))
    place = lax.axis_index("tm")
    start = pl.multiple_of(lax.rem(place, lanes // per) * per, per)
    rate = turn_ref[pl.ds(start, per), :]
    rate_ref[...] = rate
    current = got_ref[0, : 2 * per, :].astype(F32)
    out_ref[0] = current.astype(BF)
    for t in range(1, times):
        now = jnp.concatenate(
            [
                jnp.broadcast_to(rate[:, h * times + t : h * times + t + 1], (per, lanes))
                for h in range(2)
            ],
            axis=0,
        )
        current = got_ref[t, : 2 * per, :].astype(F32) + now * current
        out_ref[t] = current.astype(BF)


def backward_kernel(got_ref, rate_ref, out_ref):
    times, height, lanes = got_ref.shape
    per = height // 2
    rate = rate_ref[...]
    following = jnp.zeros((height, lanes), F32)
    out_ref[times - 1] = following.astype(BF)
    for t in range(times - 2, -1, -1):
        now = jnp.concatenate(
            [
                jnp.broadcast_to(rate[:, h * times + t + 1 : h * times + t + 2], (per, lanes))
                for h in range(2)
            ],
            axis=0,
        )
        following = now * (got_ref[t + 1].astype(F32) + following)
        out_ref[t] = following.astype(BF)


def setting_rows(ref, h):
    blocks, height, lanes = ref.shape
    per = height // 2
    return ref[:, h * per : (h + 1) * per, :].reshape(blocks * per, lanes)


def coupling_kernel(arrow_ref, forward_ref, out_ref):
    blocks, height, lanes = out_ref.shape
    per = height // 2
    for h in range(2):
        total = lax.dot_general(
            arrow_ref[h],
            setting_rows(forward_ref, h),
            (((0,), (0,)), ((), ())),
            preferred_element_type=F32,
        )
        out_ref[:, h * per : (h + 1) * per, :] = (-total).astype(BF).reshape(blocks, per, lanes)


def sum_kernel(got_ref, rhs_ref, out_ref):
    times, height, lanes = got_ref.shape
    total = got_ref[0].astype(F32)
    for t in range(1, times):
        total = total + got_ref[t].astype(F32)
    out_ref[...] = total
    own = rhs_ref.shape[1]
    place = lax.axis_index("space") * own
    for h in range(2):
        rows = pl.ds(h * (height // 2) + place, own)
        out_ref[rows, :] = out_ref[rows, :] + rhs_ref[h]


def settle_kernel(a_ref, b_ref, c_ref, d_ref, out_ref):
    rows = out_ref.shape[0]
    total = (a_ref[...] + b_ref[...]) + (c_ref[...] + d_ref[...])
    first = lax.rem(lax.axis_index("space"), 2) == 0
    out_ref[...] = jnp.where(first, total[:rows], total[rows:]).astype(BF)


def spread_kernel(*refs):
    out_ref = refs[-1]
    line = jnp.concatenate([ref[...] for ref in refs[:-1]], axis=0)
    out_ref[...] = jnp.broadcast_to(line[None], out_ref.shape)


def tip_kernel(got_ref, tip_ref, mine_ref, own_ref, other_ref, solved_ref, fixed_ref):
    order = tip_ref.shape[1]
    line, high, lanes = got_ref.shape
    rows = order // (line * (lax.axis_size("tm") // line))
    lines = high // rows
    outer = lax.axis_index("tm") // line
    for d in range(lines):
        start = lax.rem(outer + lines - d, lines) * line
        fixed_ref[pl.ds(start, line)] = got_ref[:, d * rows : (d + 1) * rows, :]
    core = lax.rem(lax.axis_index("space"), 2)
    row = lax.broadcasted_iota(jnp.int32, (order, order), 0)
    col = lax.broadcasted_iota(jnp.int32, (order, order), 1)
    lower = jnp.where(row >= col, tip_ref[core].astype(F32), 0.0).astype(BF)
    fixed = fixed_ref[...].reshape(order, lanes)
    inner = jnp.dot(lower, fixed, preferred_element_type=F32).astype(BF)
    solved = lax.dot_general(lower, inner, (((0,), (0,)), ((), ())), preferred_element_type=F32)
    solved_ref[...] = solved
    mine_ref[...] = solved.astype(BF)
    own = own_ref.shape[0]
    place = lax.axis_index("tm") * lax.axis_size("space") + lax.axis_index("space")
    own_ref[...] = solved_ref[pl.ds(place * own, own), :]
    other_ref[...] = solved_ref[pl.ds((place + 1 - 2 * core) * own, own), :]


def index_of(e, shift):
    place = lax.axis_index("space")
    chip, core = place // 2, lax.rem(place, 2)
    return 2 * lax.rem(chip + shift, 4) + (1 - core if e else core)


def keep_kernel(mask_ref, factor_ref, out_ref, held, sems):
    rows = held.shape[2]
    tiles = rows // TILE
    place = lax.axis_index("space")
    sources = [index_of(e, 4 - shift) for e in range(2) for shift in SHIFTS]

    def copy_in(j):
        start = pl.multiple_of(sources[j] * rows, rows)
        return pltpu.make_async_copy(
            factor_ref.at[:, :, pl.ds(start, rows)], held.at[j], sems.at[0, j]
        )

    def copy_out(j):
        return pltpu.make_async_copy(held.at[j], out_ref.at[j], sems.at[1, j])

    for j in range(8):

        @pl.when(sources[j] <= place)
        def _(j=j):
            copy_in(j).start()

    for j in range(8):

        @pl.when(sources[j] <= place)
        def _(j=j):
            copy_in(j).wait()

            @pl.loop(0, tiles * tiles)
            def _(at):
                r, c = at // tiles, lax.rem(at, tiles)
                marked = mask_ref[place * tiles + r, sources[j] * tiles + c] > 0
                dead = jnp.logical_not(marked)
                if j == 0:
                    dead = jnp.logical_or(jnp.logical_and(dead, r != c), r < c)

                @pl.when(dead)
                def _():
                    rs = pl.ds(pl.multiple_of(r * TILE, TILE), TILE)
                    cs = pl.ds(pl.multiple_of(c * TILE, TILE), TILE)
                    held[j, :, rs, cs] = jnp.zeros((2, TILE, TILE), BF)

            if j == 0:
                row = lax.broadcasted_iota(jnp.int32, (TILE, TILE), 0)
                col = lax.broadcasted_iota(jnp.int32, (TILE, TILE), 1)
                for h in range(2):
                    for r in range(tiles):
                        sl = slice(r * TILE, (r + 1) * TILE)
                        block = held[0, h, sl, sl].astype(F32)
                        held[0, h, sl, sl] = jnp.where(row >= col, block, 0.0).astype(BF)
            copy_out(j).start()

    for j in range(8):

        @pl.when(sources[j] <= place)
        def _(j=j):
            copy_out(j).wait()


def factor_kernel(*refs):
    pieces = refs[:8]
    factor_ref, keep_ref, send_ref, held, values, total, parts, sems = refs[8:]
    place = lax.axis_index("space")
    sources = [index_of(e, 4 - shift) for e in range(2) for shift in SHIFTS]

    def copies(j):
        return (
            pltpu.make_async_copy(pieces[j], values.at[j], sems.at[0, j]),
            pltpu.make_async_copy(factor_ref.at[j], held.at[j], sems.at[1, j]),
        )

    def copy_out(e, d):
        out_ref = send_ref if e else keep_ref
        return pltpu.make_async_copy(parts.at[4 * e + d], out_ref.at[d], sems.at[2, 4 * e + d])

    for j in range(8):

        @pl.when(sources[j] <= place)
        def _(j=j):
            for copy in copies(j):
                copy.start()

    for j in range(8):

        @pl.when(sources[j] <= place)
        def _(j=j):
            for copy in copies(j):
                copy.wait()
            for h in range(2):
                got = jnp.dot(
                    held[j, h], setting_rows(values.at[j], h), preferred_element_type=F32
                )
                total[h] = total[h] + got if j else got

    inner = [jnp.transpose(total[h]).astype(BF) for h in range(2)]
    for e in (1, 0):
        for d, shift in enumerate(SHIFTS):
            target = index_of(e, shift)
            at = 4 * e + SHIFTS.index((4 - shift) % 4)

            @pl.when(target <= place)
            def _(at=at, to=4 * e + d):
                for h in range(2):
                    parts[to, h] = jnp.dot(
                        inner[h], held[at, h], preferred_element_type=F32
                    ).astype(BF)

            @pl.when(target > place)
            def _(to=4 * e + d):
                parts[to] = jnp.zeros(parts.shape[1:], BF)

            copy_out(e, d).start()
    for e in (1, 0):
        for d in range(4):
            copy_out(e, d).wait()


def add_kernel(keep_ref, got_ref, *outs):
    for d, out_ref in enumerate(outs):
        out_ref[...] = keep_ref[d] + got_ref[d]


def carried_kernel(
    a_ref, b_ref, c_ref, d_ref, arrow_ref, mine_ref, other_ref, own_ref, got_ref,
    carried_ref, out_ref, both_ref, fixed_ref
):
    blocks, height, lanes = out_ref.shape
    per = height // 2
    core = lax.rem(lax.axis_index("space"), 2)
    fixed_ref[pl.ds(core, 1)] = mine_ref[...][None]
    fixed_ref[pl.ds(1 - core, 1)] = other_ref[...][None]
    both_ref[pl.ds(core, 1)] = own_ref[...][None]
    both_ref[pl.ds(1 - core, 1)] = got_ref[...][None]
    for h in range(2):
        total = (a_ref[h].astype(F32) + b_ref[h].astype(F32)) + (
            c_ref[h].astype(F32) + d_ref[h].astype(F32)
        )
        total = jnp.transpose(total)
        total = total - jnp.dot(arrow_ref[h], fixed_ref[h], preferred_element_type=F32)
        carried_ref[h] = total
        out_ref[:, h * per : (h + 1) * per, :] = total.astype(BF).reshape(blocks, per, lanes)


def final_kernel(carried_ref, following_ref, out_ref):
    count = carried_ref.shape[1]
    for h in range(2):
        out_ref[pl.ds(h, count, stride=2), :] = carried_ref[h] + setting_rows(
            following_ref, h
        ).astype(F32)


def on_device(inverse_factor, tile_mask, carry_rate, right_side, arrow_rows, fixed_rhs, tip_factor):
    times = lax.axis_size("tm")
    devices = lax.axis_size("space")
    _, count, _, lanes = right_side.shape
    per = count // times
    block = (times, 2 * per, lanes)
    fixed_total = tip_factor.shape[1]
    near = [(i, i + 1 - 2 * (i % 2)) for i in range(devices)]

    def along(shift):
        chips = devices // 2
        return [(i, 2 * ((i // 2 + shift) % chips) + i % 2) for i in range(devices)]

    def turned(array):
        return lax.all_to_all(array, "tm", 0, 0, tiled=True)

    def distant(array):
        return pltpu.with_memory_space_constraint(array, pltpu.HBM)

    far = pl.BlockSpec(memory_space=pltpu.HBM)
    packed = call(
        pack_kernel,
        pltpu.HBM((times, 2 * per + 8, lanes), BF),
        [
            pltpu.VMEM((2 * count, lanes), F32),
            pltpu.VMEM((2, count), F32),
            pltpu.VMEM((times, 2 * per + 8, lanes), BF),
            pltpu.SemaphoreType.DMA((9,)),
        ],
        in_specs=[far, far],
        out_specs=far,
    )(distant(right_side.reshape(2 * count, lanes)), distant(jnp.transpose(carry_rate[0])))
    packed, tile_mask = lax.optimization_barrier((packed, tile_mask))
    held = call(
        keep_kernel,
        pltpu.HBM((8, 2, count, count), BF),
        [pltpu.VMEM((8, 2, count, count), BF), pltpu.SemaphoreType.DMA((2, 8))],
        in_specs=[pl.BlockSpec(memory_space=pltpu.SMEM), far],
        out_specs=far,
        vmem=12,
        moved=16 * MIB,
    )(tile_mask, distant(inverse_factor[:, 0]))
    packed, held = lax.optimization_barrier((turned(packed), held))
    forward, rate = call(
        forward_kernel,
        (shape(block, BF), shape((per, lanes), F32)),
        [pltpu.VMEM((8 * times, lanes), F32), pltpu.VMEM((lanes, lanes), F32)],
    )(packed)
    forward_b = turned(forward)

    pieces = [forward_b] + [lax.ppermute(forward_b, "space", along(s)) for s in SHIFTS[1:]]
    arrow_rows, forward_b = lax.optimization_barrier((arrow_rows, forward_b))
    arrow = jnp.transpose(arrow_rows[0], (1, 0, 2))
    coupling = call(
        coupling_kernel,
        shape((times, 2 * fixed_total // times, lanes), BF),
        flops=1 << 32,
        moved=8 * MIB,
    )(arrow, forward_b)
    sums = call(sum_kernel, shape((2 * fixed_total // times, lanes), F32))(
        turned(coupling), fixed_rhs
    )
    pieces = pieces + [lax.ppermute(p, "space", near) for p in pieces]
    sums = sums + lax.ppermute(sums, "space", near)
    pieces, sums = lax.optimization_barrier((pieces, sums))
    fixed = [sums] + [lax.ppermute(sums, "space", along(s)) for s in SHIFTS[1:]]
    part = (2, lanes, count)
    keep, send = call(
        factor_kernel,
        (shape((4,) + part, BF), shape((4,) + part, BF)),
        [
            pltpu.VMEM((8, 2, count, count), BF),
            pltpu.VMEM((8,) + block, BF),
            pltpu.VMEM((2, count, lanes), F32),
            pltpu.VMEM((8,) + part, BF),
            pltpu.SemaphoreType.DMA((3, 8)),
        ],
        in_specs=[far] * 9,
        out_specs=(far, far),
        vmem=24,
        flops=1 << 31,
        moved=12 * MIB,
    )(*[distant(p) for p in pieces], distant(held))
    send, fixed = lax.optimization_barrier((send, fixed))
    chunk = (sums.shape[0] // 2, lanes)
    settled = call(settle_kernel, shape(chunk, BF))(*fixed)
    parts = call(add_kernel, (shape(part, BF),) * 4, vmem=8)(keep, lax.ppermute(send, "space", near))

    line = 8
    lines = times // line
    inner = [[y * line + z for z in range(line)] for y in range(lines)]
    chunks = [settled]
    for d in range(1, lines):
        pairs = [(i, (i + d * line) % times) for i in range(times)]
        chunks.append(lax.ppermute(settled, "tm", pairs))
    chunks, parts = lax.optimization_barrier((chunks, parts))
    scaled = [parts[0]] + [lax.ppermute(p, "space", along(s)) for p, s in zip(parts[1:], SHIFTS[1:])]
    spread = call(spread_kernel, shape((line, lines * chunk[0], lanes), BF))(*chunks)
    got = lax.all_to_all(spread, "tm", 0, 0, axis_index_groups=inner, tiled=True)
    own = (fixed_rhs.shape[1], lanes)
    mine, own_rows, other_rows = call(
        tip_kernel,
        (shape((fixed_total, lanes), BF), shape(own, F32), shape(own, F32)),
        [pltpu.VMEM((fixed_total, lanes), F32), pltpu.VMEM((times,) + chunk, BF)],
    )(got, tip_factor)
    carried, ready, fixed_own = call(
        carried_kernel,
        (shape((2, count, lanes), F32), shape(block, BF), shape(fixed_rhs.shape, F32)),
        [pltpu.VMEM((2, fixed_total, lanes), BF)],
    )(
        *scaled,
        arrow,
        mine,
        lax.ppermute(mine, "space", near),
        own_rows,
        lax.ppermute(other_rows, "space", near),
    )
    following = turned(call(backward_kernel, shape(block, BF))(turned(ready), rate))
    solution = call(final_kernel, shape((2 * count, lanes), F32))(carried, following)
    return (solution.reshape(right_side.shape), fixed_own)


def solution(mesh):
    placed = (
        P(None, "tm", "space", None),
        P(),
        P("tm", "space", None),
        P("tm", "space", None, None),
        P("tm", "space", None, None),
        P(None, ("tm", "space"), None),
        P(),
    )
    return jax.shard_map(
        on_device,
        mesh=mesh,
        in_specs=placed,
        out_specs=(P("tm", "space", None, None), P(None, ("tm", "space"), None)),
        check_vma=False,
    )
```
